32 devices in a mesh: groups: 2 (over x), slab: 16 (over z, y, core).
Axes of the slice: x: 2, y: 2, z: 4, core: 2. Of those that a mesh axis runs over, the one named last changes fastest.
Arguments:
- activations: bfloat16 [2048, 65536], P(('groups', 'slab')), parts along dimension 0, may hold values from 0 to 4
- weights: bfloat16 [6, 2, 512, 128, 128], P(None, None, 'slab'), may hold values from -0.5 to 0.5
- biases: float32 [6, 65536], P(None, 'slab'), may hold values from -1 to 0.5
- columns: int32 [6, 512], P(None, 'slab'), may hold values from 0 to 31
Outputs:
- features: bfloat16 [2048, 65536], P(('groups', 'slab')), parts along dimension 0
The draws below stay inside these ranges and needn't reach their ends.
There are 2 independent parts, one for each index of `groups`. The reference program is written for one: setup_inputs(seed, part) draws one part's arguments, and reference() takes and returns one part's arrays. A program takes and returns all parts, laid end to end along the dimension named above; an argument that names none is the same for every part. Nothing has to cross between parts.
Inputs may be any that keep to these rules, and one draw needn't show every extreme that they name: columns name a block within a group of 32 consecutive blocks.
All inputs are finite; a program needn't handle non-finite values.
Results may differ from the reference program's by a relative error of at most 0.0072.
Values may be sent and summed in bfloat16 or wider, within the bound.
No kernel may reach another device: no remote copies, remote signals or barrier semaphores. Data moves between devices by JAX's collectives and lax.ppermute only.
A program may use at most 128 MiB of HBM per device.

```python
import jax
import jax.numpy as jnp

NEURONS = 65536
BLK = 128
LAYERS = 6
ROWS = 1024
BLOCKS = 512
BPD = 32
N_SLAB = 16


def touch_ends(entries, stream_key, least, largest):
    longest = entries.shape.index(max(entries.shape))
    spots = []
    for shift in (0, 1):
        where = [jax.random.randint(jax.random.fold_in(stream_key, axis), (), 0, length) for axis, length in enumerate(entries.shape)]
        where[longest] = (where[longest] + shift) % entries.shape[longest]
        spots.append(tuple(where))
    return entries.at[spots[0]].set(least).at[spots[1]].set(largest)


def block_levels(stream_key, extent, pieces, smallest, top_value):
    loudness, own = 1.0, jax.random.fold_in(stream_key, 6)
    for position, shards_of in pieces:
        heights = jnp.exp(jax.random.uniform(jax.random.fold_in(own, position), (shards_of,), jnp.float32, smallest / len(pieces), top_value / len(pieces)))
        loudness = loudness * jnp.repeat(heights, extent[position] // shards_of).reshape([-1 if axis == position else 1 for axis in range(len(extent))])
    return loudness


def gaussian(key, shape, width, reach, split=(), kind=jnp.bfloat16):
    entries = jax.random.normal(key, shape, jnp.float32) * width
    if len(split) > 0:
        entries = block_levels(key, shape, split, -0.22, 0.18) * entries
    return jnp.clip(entries, min=-reach, max=reach).astype(kind)


def setup_inputs(seed: int = 0, part: int = 0) -> dict:
    splits = jax.random.split(jax.random.key(seed), 5)
    own_keys = jax.random.split(jax.random.fold_in(splits[4], part), 5)
    return {
        "activations": jnp.clip(4.0 * jax.random.uniform(own_keys[0], (ROWS, NEURONS), jnp.float32) ** block_levels(own_keys[0], (ROWS, NEURONS), ((0, 16),), -0.2, 0.2), 0.0, 4.0).astype(jnp.bfloat16),
        "weights": gaussian(splits[1], (LAYERS, 2, BLOCKS, BLK, BLK), BLK ** -0.5, 0.5, ((2, 16),)),
        "biases": jnp.clip(-1.0 + 1.5 * jax.random.uniform(splits[2], (LAYERS, NEURONS), jnp.float32) ** block_levels(splits[2], (LAYERS, NEURONS), ((1, 16),), -0.2, 0.2), -1.0, 0.5),
        "columns": touch_ends(jax.random.randint(splits[3], (LAYERS, BLOCKS), 0, BPD), jax.random.fold_in(splits[3], 1), 0, BPD - 1).astype(jnp.int32),
    }


ceiling = 4.0


def section_bit(section, remote, log_count):
    if remote <= 1:
        return log_count - 1
    return ((remote - 1 - section) * (log_count - 1)) // (remote - 1)


def reference(activations, weights, biases, columns):
    block_count = NEURONS // BLK
    per_device = block_count // N_SLAB
    log_count = N_SLAB.bit_length() - 1
    remote = (LAYERS + 1) // 2
    current = activations.reshape(ROWS, block_count, BLK)
    home_slab = (jnp.arange(block_count, dtype=jnp.int32) // per_device).astype(jnp.int32)
    for layer_index in range(LAYERS):
        if layer_index % 2 == 0:
            shifted = jnp.int32(1 << section_bit(layer_index // 2, remote, log_count))
            owner_slab = jnp.bitwise_xor(home_slab, shifted).astype(jnp.int32)
        else:
            owner_slab = home_slab
        source = (owner_slab * per_device + columns[layer_index].astype(jnp.int32)).astype(jnp.int32)
        crossing = jnp.take(current, source, axis=1)
        summed = jnp.einsum("rkb,kbc->rkc", current.astype(jnp.float32), weights[layer_index, 0].astype(jnp.float32))
        summed = summed + jnp.einsum("rkb,kbc->rkc", crossing.astype(jnp.float32), weights[layer_index, 1].astype(jnp.float32))
        summed = summed + biases[layer_index].reshape(block_count, BLK)
        current = jnp.clip(summed, 0.0, ceiling).astype(jnp.bfloat16)
    return current.reshape(ROWS, NEURONS)
```

```python
import functools

import jax
import jax.numpy as jnp
from jax import lax
from jax.experimental import pallas as pl
from jax.experimental.pallas import tpu as pltpu
from jax.sharding import PartitionSpec as P

ceiling = 4.0


def swap(block, axis, offset):
    count = lax.axis_size(axis)
    return lax.ppermute(block, axis, [(i, i ^ offset) for i in range(count)])


def section_bit(section, remote, log_count):
    if remote <= 1:
        return log_count - 1
    return (remote - 1 - section) * (log_count - 1) // (remote - 1)


def split_kernel(offsets, first_bit, me_ref, act_ref, *refs):
    count = len(offsets)
    outs, taken, sems = refs[:count], refs[count], refs[count + 1]
    width = taken.shape[-1]
    half = pl.program_id(0)

    def copy(h, j):
        home = me_ref[0] ^ (offsets[j] | (h << first_bit))
        start = pl.multiple_of(home * width, 128)
        return pltpu.make_async_copy(
            act_ref.at[:, pl.ds(start, width)], taken.at[h, j], sems.at[h, j]
        )

    @pl.when(half == 0)
    def _():
        for h in range(2):
            for j in range(count):
                copy(h, j).start()

    for j in range(count):
        copy(half, j).wait()
        for k in range(width // 128):
            outs[j][0, k] = taken[half, j, :, k * 128 : (k + 1) * 128]


def split(me, activations, offsets, first_bit, blocks):
    rows = activations.shape[0]
    count = len(offsets)
    width = blocks * 128
    piece = jax.ShapeDtypeStruct((2, blocks, rows, 128), activations.dtype)
    return pl.pallas_call(
        functools.partial(split_kernel, offsets, first_bit),
        out_shape=[piece] * count,
        grid_spec=pltpu.PrefetchScalarGridSpec(
            num_scalar_prefetch=1,
            grid=(2,),
            in_specs=[pl.BlockSpec(memory_space=pl.ANY)],
            out_specs=[pl.BlockSpec((1, blocks, rows, 128), lambda h, me: (h, 0, 0, 0))] * count,
            scratch_shapes=[
                pltpu.VMEM((2, count, rows, width), activations.dtype),
                pltpu.SemaphoreType.DMA((2, count)),
            ],
        ),
        cost_estimate=pl.CostEstimate(
            flops=0, transcendentals=0, bytes_accessed=4 * activations.size
        ),
        name="split",
    )(me, activations)


def merge_kernel(offsets, first_bit, first_row, aliased, me_ref, *refs):
    count = len(offsets)
    pieces = refs[:count]
    out_ref, placed, sems = refs[count + aliased :]
    rows, width = placed.shape[-2:]
    half = pl.program_id(0)

    def copy(h, j):
        home = me_ref[0] ^ (offsets[j] | (h << first_bit))
        start = pl.multiple_of(home * width, 128)
        return pltpu.make_async_copy(
            placed.at[h, j],
            out_ref.at[pl.ds(first_row, rows), pl.ds(start, width)],
            sems.at[h, j],
        )

    for j in range(count):
        for k in range(width // 128):
            placed[half, j, :, k * 128 : (k + 1) * 128] = pieces[j][0, k]
        copy(half, j).start()

    @pl.when(half == 1)
    def _():
        for h in range(2):
            for j in range(count):
                copy(h, j).wait()


def merge(me, pieces, offsets, first_bit, first_row, total_rows, into):
    count = len(offsets)
    _, blocks, rows, _ = pieces[0].shape
    width = blocks * 128
    aliased = 0 if into is None else 1
    more = [] if into is None else [into]
    return pl.pallas_call(
        functools.partial(merge_kernel, offsets, first_bit, first_row, aliased),
        out_shape=jax.ShapeDtypeStruct((total_rows, 2 * count * width), pieces[0].dtype),
        grid_spec=pltpu.PrefetchScalarGridSpec(
            num_scalar_prefetch=1,
            grid=(2,),
            in_specs=[pl.BlockSpec((1, blocks, rows, 128), lambda h, me: (h, 0, 0, 0))] * count
            + [pl.BlockSpec(memory_space=pl.ANY)] * aliased,
            out_specs=pl.BlockSpec(memory_space=pl.ANY),
            scratch_shapes=[
                pltpu.VMEM((2, count, rows, width), pieces[0].dtype),
                pltpu.SemaphoreType.DMA((2, count)),
            ],
        ),
        input_output_aliases={1 + count: 0} if aliased else {},
        cost_estimate=pl.CostEstimate(
            flops=0, transcendentals=0, bytes_accessed=8 * count * pieces[0].size
        ),
        name="merge",
    )(me, *pieces, *more)


def layers_kernel(plan, cols_ref, me_ref, *refs):
    sources, crossed, step, flip, split_out, layer, blocks = plan
    refs = list(refs)
    src = [refs.pop(0) for _ in range(sources)]
    other = refs.pop(0) if crossed else None
    own_w = refs.pop(0)
    far_w = [[refs.pop(0), refs.pop(0)] for _ in range(2)]
    bias = refs.pop(0)
    middle = refs.pop()
    outs = refs
    phase, at = pl.program_id(0), pl.program_id(1)
    count, _, _, rows, _ = middle.shape

    def joined(ref, g, k, order=None):
        if order is None:
            return ref[:, g, k].reshape(count * rows, 128)
        return jnp.concatenate([ref[j, g, k] for j in order], axis=0)

    def from_source(g, k):
        if sources == 1:
            return joined(src[0], g, k)
        return jnp.concatenate([piece[g, k] for piece in src], axis=0)

    def from_partner(g, k):
        if other is None:
            return from_source(1 - g, k)
        return joined(other, g, k, [j ^ flip for j in range(count)])

    def run(p, own_of, partner_of, store):
        for g in range(2):
            for t in range(step):
                k = at * step + t
                c = cols_ref[((layer + p) * 2 + g) * blocks + k]
                both = jnp.concatenate([own_of(g, k), partner_of(g, c)], axis=1)
                if g == 0:
                    w = jnp.concatenate([own_w[0, 0, t], own_w[0, 1, t]], axis=0)
                else:
                    w = jnp.concatenate([far_w[p][0][t], far_w[p][1][t]], axis=0)
                summed = jnp.dot(both, w, preferred_element_type=jnp.float32)
                summed = summed + bias[0, g, t]
                store(g, k, t, jnp.clip(summed, 0.0, ceiling).astype(jnp.bfloat16))

    @pl.when(phase == 0)
    def _():
        def store(g, k, t, value):
            middle[:, g, k] = value.reshape(count, rows, 128)

        run(0, from_source, from_partner, store)

    @pl.when(phase == 1)
    def _():
        def store(g, k, t, value):
            if split_out:
                for j in range(count):
                    outs[j][g, t] = value[j * rows : (j + 1) * rows]
            else:
                outs[0][:, g, t] = value.reshape(count, rows, 128)

        def own(g, k):
            return joined(middle, g, k)

        run(1, own, own, store)


def two_layers(
    cols, me, source, other, weights, far, biases, layer, chunk, rows, count, flip, split_out, name
):
    blocks = weights.shape[2]
    part = far[0].shape[0] // lax.axis_size("groups")
    step = min(8, part, blocks)
    steps = blocks // step

    def far_spec(p, which):
        def index(phase, at, cols, me):
            at = jnp.where(phase == p, at, (steps - 1) if p == 0 else 0)
            first = which * blocks + at * step
            return (((first // part) ^ me[1]) * (part // step) + (first % part) // step, 0, 0)

        return pl.BlockSpec((step, 128, 128), index)

    whole = pl.BlockSpec((count, 2, blocks, rows, 128), lambda p, a, c, m: (0, 0, 0, 0, 0))
    if len(source) > 1:
        specs = [
            pl.BlockSpec((2, blocks, rows, 128), lambda p, a, c, m: (0, 0, chunk, 0))
        ] * count
    else:
        specs = [whole]
    operands = list(source)
    if other is not None:
        specs.append(whole)
        operands.append(other)
    specs.append(
        pl.BlockSpec((1, 2, step, 128, 128), lambda p, a, c, m: (layer + p, 0, a, 0, 0))
    )
    operands.append(weights)
    for p in range(2):
        for which in range(2):
            specs.append(far_spec(p, which))
            operands.append(far[p])
    specs.append(pl.BlockSpec((1, 2, step, 1, 128), lambda p, a, c, m: (layer + p, 0, a, 0, 0)))
    operands.append(biases)
    if split_out:
        out_shape = [jax.ShapeDtypeStruct((2, blocks, rows, 128), jnp.bfloat16)] * count
        out_specs = [
            pl.BlockSpec((2, step, rows, 128), lambda p, a, c, m: (0, a * p, 0, 0))
        ] * count
    else:
        out_shape = [jax.ShapeDtypeStruct((count, 2, blocks, rows, 128), jnp.bfloat16)]
        out_specs = [
            pl.BlockSpec((count, 2, step, rows, 128), lambda p, a, c, m: (0, 0, a * p, 0, 0))
        ]
    plan = (len(source), other is not None, step, flip, split_out, layer, blocks)
    cells = count * rows * 2 * blocks
    return pl.pallas_call(
        functools.partial(layers_kernel, plan),
        out_shape=out_shape,
        grid_spec=pltpu.PrefetchScalarGridSpec(
            num_scalar_prefetch=2,
            grid=(2, steps),
            in_specs=specs,
            out_specs=out_specs,
            scratch_shapes=[pltpu.VMEM((count, 2, blocks, rows, 128), jnp.bfloat16)],
        ),
        cost_estimate=pl.CostEstimate(
            flops=2 * 2 * cells * 256 * 128,
            transcendentals=0,
            bytes_accessed=2 * 3 * cells * 128 + 8 * blocks * 2 * 128 * 128 * 2,
        ),
        name=name,
    )(cols, me, *operands)


def local(activations, weights, biases, columns):
    slab_count, group_count = lax.axis_size("slab"), lax.axis_size("groups")
    log_count = slab_count.bit_length() - 1
    layer_count, _, blocks, width, _ = weights.shape
    local_rows = activations.shape[0]
    remote = (layer_count + 1) // 2
    bits = [section_bit(m, remote, log_count) for m in range(remote)]
    first_bit = bits[0]
    spread = [b for b in range(log_count) if b != first_bit]
    count = slab_count // 2
    offsets = [
        sum(((j >> i) & 1) << b for i, b in enumerate(spread)) for j in range(count)
    ]
    chunks = 2 if local_rows % 32 == 0 else 1
    rows = local_rows // chunks
    slab, group = lax.axis_index("slab"), lax.axis_index("groups")
    me = jnp.stack([slab, group]).astype(jnp.int32)

    part = 2 * blocks // group_count

    def fetch(layer):
        flat = weights[layer].reshape(2 * blocks, width, width)
        mine = lax.dynamic_slice_in_dim(flat, group * part, part, axis=0)
        return swap(mine, "slab", 1 << first_bit)

    def share(mine):
        held = [mine]
        for b in range(group_count.bit_length() - 1):
            held = held + [swap(one, "groups", 1 << b) for one in held]
        return jnp.concatenate(held, axis=0)

    far = [share(fetch(layer)) for layer in range(layer_count)]
    far_bias = swap(biases, "slab", 1 << first_bit)
    far_columns = swap(columns, "slab", 1 << first_bit)
    bias = jnp.stack([biases, far_bias], axis=1).reshape(layer_count, 2, blocks, 1, width)
    cols = jnp.stack([columns, far_columns], axis=1).reshape(-1)

    pieces = split(me, activations, offsets, first_bit, blocks)
    pieces = [pieces[0]] + [swap(pieces[j], "slab", offsets[j]) for j in range(1, count)]

    output = None
    done = []
    for chunk in range(chunks):
        source, other, flip = pieces, None, 0
        for m in range(remote):
            if m > 0:
                other = swap(source[0], "slab", 1 << bits[m])
                flip = offsets.index(1 << bits[m])
            last = m == remote - 1
            source = two_layers(
                cols, me, source, other, weights, far[2 * m : 2 * m + 2], bias,
                2 * m, chunk, rows, count, flip, last, f"layers{2 * m}_chunk{chunk}",
            )
        done.append([source[0]] + [swap(source[j], "slab", offsets[j]) for j in range(1, count)])
    for chunk in range(chunks):
        output = merge(
            me, done[chunk], offsets, first_bit, chunk * rows, local_rows, output
        )
    return output


def solution(mesh):
    placed = (
        P(("groups", "slab"), None),
        P(None, None, "slab", None, None),
        P(None, "slab"),
        P(None, "slab"),
    )
    return jax.shard_map(
        local, mesh=mesh, in_specs=placed, out_specs=P(("groups", "slab"), None), check_vma=False
    )
```

```python
import functools

import jax
import jax.numpy as jnp
from jax import lax
from jax.experimental import pallas as pl
from jax.experimental.pallas import tpu as pltpu
from jax.sharding import PartitionSpec as P


ceiling = 4.0


def swap(block, axis, offset):
    count = lax.axis_size(axis)
    return lax.ppermute(block, axis, [(i, i ^ offset) for i in range(count)])


def section_bit(section, remote, log_count):
    if remote <= 1:
        return log_count - 1
    return (remote - 1 - section) * (log_count - 1) // (remote - 1)


def split_kernel(offsets, first_bit, me_ref, act_ref, *refs):
    count = len(offsets)
    outs, taken, sems = refs[:count], refs[count], refs[count + 1]
    width = taken.shape[-1]
    half = pl.program_id(0)

    def copy(h, j):
        home = me_ref[0] ^ (offsets[j] | (h << first_bit))
        start = pl.multiple_of(home * width, 128)
        return pltpu.make_async_copy(
            act_ref.at[:, pl.ds(start, width)], taken.at[h, j], sems.at[h, j]
        )

    @pl.when(half == 0)
    def _():
        for h in range(2):
            for j in range(count):
                copy(h, j).start()

    for j in range(count):
        copy(half, j).wait()
        for k in range(width // 128):
            outs[j][0, k] = taken[half, j, :, k * 128 : (k + 1) * 128]


def split(me, activations, offsets, first_bit, blocks):
    rows = activations.shape[0]
    count = len(offsets)
    width = blocks * 128
    piece = jax.ShapeDtypeStruct((2, blocks, rows, 128), activations.dtype)
    return pl.pallas_call(
        functools.partial(split_kernel, offsets, first_bit),
        out_shape=[piece] * count,
        grid_spec=pltpu.PrefetchScalarGridSpec(
            num_scalar_prefetch=1,
            grid=(2,),
            in_specs=[pl.BlockSpec(memory_space=pl.ANY)],
            out_specs=[pl.BlockSpec((1, blocks, rows, 128), lambda h, me: (h, 0, 0, 0))] * count,
            scratch_shapes=[
                pltpu.VMEM((2, count, rows, width), activations.dtype),
                pltpu.SemaphoreType.DMA((2, count)),
            ],
        ),
        cost_estimate=pl.CostEstimate(
            flops=0, transcendentals=0, bytes_accessed=4 * activations.size
        ),
        name="split",
    )(me, activations)


def merge_kernel(offsets, half_bit, aliased, me_ref, *refs):
    count = len(offsets)
    pieces = refs[:count]
    out_ref, placed, sems = refs[count + aliased :]
    width = placed.shape[-1]
    step = pl.program_id(0)
    last = pl.num_programs(0) - 1
    rows = placed.shape[-2]

    def copy(at, j):
        home = me_ref[0] ^ (offsets[j] | half_bit)
        start = pl.multiple_of(home * width, 128)
        return pltpu.make_async_copy(
            placed.at[at, j],
            out_ref.at[pl.ds(at * rows, rows), pl.ds(start, width)],
            sems.at[at, j],
        )

    for j in range(count):
        for k in range(width // 128):
            placed[step, j, :, k * 128 : (k + 1) * 128] = pieces[j][k]
        copy(step, j).start()

    @pl.when(step == last)
    def _():
        for at in range(placed.shape[0]):
            for j in range(count):
                copy(at, j).wait()


def merge(me, pieces, offsets, half_bit, into):
    count = len(offsets)
    blocks, total_rows, _ = pieces[0].shape
    steps = 2 if total_rows % 32 == 0 else 1
    rows = total_rows // steps
    width = blocks * 128
    aliased = 0 if into is None else 1
    more = [] if into is None else [into]
    return pl.pallas_call(
        functools.partial(merge_kernel, offsets, half_bit, aliased),
        out_shape=jax.ShapeDtypeStruct((total_rows, 2 * count * width), pieces[0].dtype),
        grid_spec=pltpu.PrefetchScalarGridSpec(
            num_scalar_prefetch=1,
            grid=(steps,),
            in_specs=[pl.BlockSpec((blocks, rows, 128), lambda i, me: (0, i, 0))] * count
            + [pl.BlockSpec(memory_space=pl.ANY)] * aliased,
            out_specs=pl.BlockSpec(memory_space=pl.ANY),
            scratch_shapes=[
                pltpu.VMEM((steps, count, rows, width), pieces[0].dtype),
                pltpu.SemaphoreType.DMA((steps, count)),
            ],
        ),
        input_output_aliases={1 + count: 0} if aliased else {},
        cost_estimate=pl.CostEstimate(
            flops=0, transcendentals=0, bytes_accessed=4 * count * pieces[0].size
        ),
    )(me, *pieces, *more)


def layers_kernel(plan, cols_ref, me_ref, *refs):
    sources, half, flip, joined_out, step, layer, blocks = plan
    refs = list(refs)
    src = [refs.pop(0) for _ in range(sources)]
    other = refs.pop(0) if sources == 1 else None
    w = [[refs.pop(0), refs.pop(0)] for _ in range(2)]
    bias = refs.pop(0)
    middle = refs.pop()
    outs = refs
    phase, at = pl.program_id(0), pl.program_id(1)
    count, _, rows, _ = middle.shape

    def whole(ref, k):
        return ref[:, k].reshape(count * rows, 128)

    def from_source(k):
        if sources == 1:
            return whole(src[0], k)
        return jnp.concatenate([piece[half, k] for piece in src], axis=0)

    def from_partner(k):
        if sources > 1:
            return jnp.concatenate([piece[1 - half, k] for piece in src], axis=0)
        return jnp.concatenate([other[j ^ flip, k] for j in range(count)], axis=0)

    def from_middle(k):
        return whole(middle, k)

    def run(p, own_of, partner_of, store):
        for t in range(step):
            k = at * step + t
            c = cols_ref[((layer + p) * 2 + half) * blocks + k]
            both = jnp.concatenate([own_of(k), partner_of(c)], axis=1)
            taken = jnp.concatenate([w[p][0][0, t], w[p][1][0, t]], axis=0)
            summed = jnp.dot(both, taken, preferred_element_type=jnp.float32)
            summed = summed + bias[0, 0, t]
            store(k, t, jnp.clip(summed, 0.0, ceiling).astype(jnp.bfloat16))

    @pl.when(phase == 0)
    def _():
        def store(k, t, value):
            middle[:, k] = value.reshape(count, rows, 128)

        run(0, from_source, from_partner, store)

    @pl.when(phase == 1)
    def _():
        def store(k, t, value):
            if joined_out:
                outs[0][:, t] = value.reshape(count, rows, 128)
            else:
                for j in range(count):
                    outs[j][t] = value[j * rows : (j + 1) * rows]

        run(1, from_middle, from_middle, store)


def two_layers(
    cols, me, source, other, weights, far, biases, layer, half, rows, count, flip, joined_out
):
    blocks = biases.shape[2]
    part = weights.shape[2]
    step = min(8, part, blocks)
    steps = blocks // step

    def weight_spec(p, which):
        def index(phase, at, cols, me):
            at = jnp.where(phase == p, at, (steps - 1) if p == 0 else 0)
            first = which * blocks + at * step
            piece, row = first // part, (first % part) // step
            if half == 0:
                return (layer + p, piece * (part // step) + row, 0, 0)
            return (far[p][1], (piece ^ me[1]) * (part // step) + row, 0, 0)

        return pl.BlockSpec((1, step, 128, 128), index)

    if other is None:
        specs = [pl.BlockSpec((2, blocks, rows, 128), lambda p, a, c, m: (0, 0, 0, 0))] * count
        operands = list(source)
    else:
        specs = [pl.BlockSpec((count, blocks, rows, 128), lambda p, a, c, m: (0, 0, 0, 0))] * 2
        operands = [source, other]
    own = weights.reshape(weights.shape[0], 2 * blocks, 128, 128)
    for p in range(2):
        for which in range(2):
            specs.append(weight_spec(p, which))
            operands.append(own if half == 0 else far[p][0])
    specs.append(pl.BlockSpec((1, 1, step, 1, 128), lambda p, a, c, m: (layer + p, half, a, 0, 0)))
    operands.append(biases)
    if joined_out:
        out_shape = jax.ShapeDtypeStruct((count, blocks, rows, 128), jnp.bfloat16)
        out_specs = pl.BlockSpec((count, step, rows, 128), lambda p, a, c, m: (0, a * p, 0, 0))
    else:
        out_shape = [jax.ShapeDtypeStruct((blocks, rows, 128), jnp.bfloat16)] * count
        out_specs = [pl.BlockSpec((step, rows, 128), lambda p, a, c, m: (a * p, 0, 0))] * count
    plan = (1 if other is not None else count, half, flip, joined_out, step, layer, blocks)
    cells = count * rows * blocks
    return pl.pallas_call(
        functools.partial(layers_kernel, plan),
        out_shape=out_shape,
        grid_spec=pltpu.PrefetchScalarGridSpec(
            num_scalar_prefetch=2,
            grid=(2, steps),
            in_specs=specs,
            out_specs=out_specs,
            scratch_shapes=[pltpu.VMEM((count, blocks, rows, 128), jnp.bfloat16)],
        ),
        cost_estimate=pl.CostEstimate(
            flops=2 * 2 * cells * 256 * 128,
            transcendentals=0,
            bytes_accessed=2 * 3 * cells * 128 + 2 * 2 * blocks * 128 * 128 * 2,
        ),
    )(cols, me, *operands)


def far_batches(layer_count):
    return [(l, 2) for l in range(0, layer_count - 2, 2)] + [
        (layer_count - 2, 1),
        (layer_count - 1, 1),
    ]


def local(activations, weights, biases, columns):
    slab_count, group_count = lax.axis_size("slab"), lax.axis_size("groups")
    log_count = slab_count.bit_length() - 1
    layer_count, _, blocks, width, _ = weights.shape
    rows = activations.shape[0]
    remote = (layer_count + 1) // 2
    bits = [section_bit(m, remote, log_count) for m in range(remote)]
    first_bit = bits[0]
    spread = [b for b in range(log_count) if b != first_bit]
    count = slab_count // 2
    offsets = [
        sum(((j >> i) & 1) << b for i, b in enumerate(spread)) for j in range(count)
    ]
    slab, group = lax.axis_index("slab"), lax.axis_index("groups")
    me = jnp.stack([slab, group]).astype(jnp.int32)

    mine = split(me, activations, offsets, first_bit, blocks)
    pieces = [mine[0]]
    for j in range(1, count):
        pieces.append(swap(mine[j], "slab", offsets[j]))

    far_bias = swap(biases, "slab", 1 << first_bit)
    far_columns = swap(columns, "slab", 1 << first_bit)
    bias = jnp.stack([biases, far_bias], axis=1).reshape(layer_count, 2, blocks, 1, width)
    cols = jnp.stack([columns, far_columns], axis=1).reshape(-1)

    part = 2 * blocks // group_count
    parts = weights.reshape(layer_count, group_count, part, width, width)
    far = []
    for first, size in far_batches(layer_count):
        part_mine = lax.dynamic_slice(
            parts, (first, group, 0, 0, 0), (size, 1, part, width, width)
        ).reshape(size, part, width, width)
        held = [swap(part_mine, "slab", 1 << first_bit)]
        for b in range(group_count.bit_length() - 1):
            got = []
            for one in held:
                got.append(swap(one, "groups", 1 << b))
            held = held + got
        joined = jnp.concatenate(held, axis=1)
        far += [(joined, i) for i in range(size)]

    def weights_of(half, layer):
        return [None, None] if half == 0 else far[layer : layer + 2]

    halves = [pieces, pieces]
    for m in range(remote):
        last = m == remote - 1
        for half in range(2):
            other, flip = None, 0
            if m > 0:
                other = swap(halves[half], "slab", 1 << bits[m])
                flip = offsets.index(1 << bits[m])
            halves[half] = two_layers(
                cols, me, halves[half], other, parts, weights_of(half, 2 * m), bias,
                2 * m, half, rows, count, flip, not last,
            )
    output = None
    for half in range(2):
        back = [halves[half][0]]
        for j in range(1, count):
            back.append(swap(halves[half][j], "slab", offsets[j]))
        output = merge(me, back, offsets, half << first_bit, output)
    return output


def solution(mesh):
    placed = (
        P(("groups", "slab"), None),
        P(None, None, "slab", None, None),
        P(None, "slab"),
        P(None, "slab"),
    )

    return jax.shard_map(
        local, mesh=mesh, in_specs=placed, out_specs=P(("groups", "slab"), None), check_vma=False
    )
```

```python
import functools

import jax
import jax.numpy as jnp
from jax import lax
from jax.experimental import pallas as pl
from jax.experimental.pallas import tpu as pltpu
from jax.sharding import PartitionSpec as P


ceiling = 4.0


def swap(block, axis, offset):
    count = lax.axis_size(axis)
    return lax.ppermute(block, axis, [(i, i ^ offset) for i in range(count)])


def section_bit(section, remote, log_count):
    if remote <= 1:
        return log_count - 1
    return (remote - 1 - section) * (log_count - 1) // (remote - 1)


def split_kernel(offsets, first_bit, me_ref, act_ref, *refs):
    count = len(offsets)
    outs, taken, sems = refs[:count], refs[count], refs[count + 1]
    width = taken.shape[-1]
    half = pl.program_id(0)

    def copy(h, j):
        home = me_ref[0] ^ (offsets[j] | (h << first_bit))
        start = pl.multiple_of(home * width, 128)
        return pltpu.make_async_copy(
            act_ref.at[:, pl.ds(start, width)], taken.at[h, j], sems.at[h, j]
        )

    @pl.when(half == 0)
    def _():
        for h in range(2):
            for j in range(count):
                copy(h, j).start()

    for j in range(count):
        copy(half, j).wait()
        for k in range(width // 128):
            outs[j][0, k] = taken[half, j, :, k * 128 : (k + 1) * 128]


def split(me, activations, offsets, first_bit, blocks):
    rows = activations.shape[0]
    count = len(offsets)
    width = blocks * 128
    piece = jax.ShapeDtypeStruct((2, blocks, rows, 128), activations.dtype)
    return pl.pallas_call(
        functools.partial(split_kernel, offsets, first_bit),
        out_shape=[piece] * count,
        grid_spec=pltpu.PrefetchScalarGridSpec(
            num_scalar_prefetch=1,
            grid=(2,),
            in_specs=[pl.BlockSpec(memory_space=pl.ANY)],
            out_specs=[pl.BlockSpec((1, blocks, rows, 128), lambda h, me: (h, 0, 0, 0))] * count,
            scratch_shapes=[
                pltpu.VMEM((2, count, rows, width), activations.dtype),
                pltpu.SemaphoreType.DMA((2, count)),
            ],
        ),
        cost_estimate=pl.CostEstimate(
            flops=0, transcendentals=0, bytes_accessed=4 * activations.size
        ),
        name="split",
    )(me, activations)


def merge_kernel(offsets, half_bit, aliased, me_ref, *refs):
    count = len(offsets)
    pieces = refs[:count]
    out_ref, placed, sems = refs[count + aliased :]
    width = placed.shape[-1]
    step = pl.program_id(0)
    last = pl.num_programs(0) - 1
    rows = placed.shape[-2]

    def copy(at, j):
        home = me_ref[0] ^ (offsets[j] | half_bit)
        start = pl.multiple_of(home * width, 128)
        return pltpu.make_async_copy(
            placed.at[at, j],
            out_ref.at[pl.ds(at * rows, rows), pl.ds(start, width)],
            sems.at[at, j],
        )

    for j in range(count):
        for k in range(width // 128):
            placed[step, j, :, k * 128 : (k + 1) * 128] = pieces[j][k]
        copy(step, j).start()

    @pl.when(step == last)
    def _():
        for at in range(placed.shape[0]):
            for j in range(count):
                copy(at, j).wait()


def merge(me, pieces, offsets, half_bit, into):
    count = len(offsets)
    blocks, total_rows, _ = pieces[0].shape
    steps = 2 if total_rows % 32 == 0 else 1
    rows = total_rows // steps
    width = blocks * 128
    aliased = 0 if into is None else 1
    more = [] if into is None else [into]
    return pl.pallas_call(
        functools.partial(merge_kernel, offsets, half_bit, aliased),
        out_shape=jax.ShapeDtypeStruct((total_rows, 2 * count * width), pieces[0].dtype),
        grid_spec=pltpu.PrefetchScalarGridSpec(
            num_scalar_prefetch=1,
            grid=(steps,),
            in_specs=[pl.BlockSpec((blocks, rows, 128), lambda i, me: (0, i, 0))] * count
            + [pl.BlockSpec(memory_space=pl.ANY)] * aliased,
            out_specs=pl.BlockSpec(memory_space=pl.ANY),
            scratch_shapes=[
                pltpu.VMEM((steps, count, rows, width), pieces[0].dtype),
                pltpu.SemaphoreType.DMA((steps, count)),
            ],
        ),
        input_output_aliases={1 + count: 0} if aliased else {},
        cost_estimate=pl.CostEstimate(
            flops=0, transcendentals=0, bytes_accessed=4 * count * pieces[0].size
        ),
    )(me, *pieces, *more)


def layers_kernel(plan, cols_ref, me_ref, *refs):
    sources, half, flip, joined_out, step, layer, blocks, paired = plan
    refs = list(refs)
    src = [refs.pop(0) for _ in range(sources)]
    other = refs.pop(0) if sources == 1 else None
    w = [[refs.pop(0), refs.pop(0)] for _ in range(2)]
    bias = refs.pop(0)
    middle = refs.pop()
    outs = refs
    phase, at = pl.program_id(0), pl.program_id(1)
    count, _, rows, _ = middle.shape
    swapped = me_ref[1] == 1

    def whole(ref, k):
        return ref[:, k].reshape(count * rows, 128)

    def from_source(k):
        if sources == 1:
            return whole(src[0], k)
        return jnp.concatenate([piece[half, k] for piece in src], axis=0)

    def from_partner(k):
        if sources > 1:
            return jnp.concatenate([piece[1 - half, k] for piece in src], axis=0)
        return jnp.concatenate([other[j ^ flip, k] for j in range(count)], axis=0)

    def from_middle(k):
        return whole(middle, k)

    def run(p, own_of, partner_of, store):
        for t in range(step):
            k = at * step + t
            c = cols_ref[(layer + p) * blocks + k]
            both = jnp.concatenate([own_of(k), partner_of(c)], axis=1)
            first, second = w[p][0][0, t], w[p][1][0, t]
            if paired:
                first, second = (
                    jnp.where(swapped, second, first),
                    jnp.where(swapped, first, second),
                )
            taken = jnp.concatenate([first, second], axis=0)
            summed = jnp.dot(both, taken, preferred_element_type=jnp.float32)
            summed = summed + bias[0, t]
            store(k, t, jnp.clip(summed, 0.0, ceiling).astype(jnp.bfloat16))

    @pl.when(phase == 0)
    def _():
        def store(k, t, value):
            middle[:, k] = value.reshape(count, rows, 128)

        run(0, from_source, from_partner, store)

    @pl.when(phase == 1)
    def _():
        def store(k, t, value):
            if joined_out:
                outs[0][:, t] = value.reshape(count, rows, 128)
            else:
                for j in range(count):
                    outs[j][t] = value[j * rows : (j + 1) * rows]

        run(1, from_middle, from_middle, store)


def two_layers(
    cols, me, source, other, weights, far, biases, layer, half, rows, count, flip, joined_out
):
    blocks = biases.shape[1]
    part = weights.shape[2]
    paired = half == 1 and len(far[0][0]) == 2
    step = min(8, part, blocks)
    steps = blocks // step

    def weight_spec(p, which):
        def index(phase, at, cols, me):
            at = jnp.where(phase == p, at, (steps - 1) if p == 0 else 0)
            if paired:
                return (far[p][1], at, 0, 0)
            first = which * blocks + at * step
            piece, row = first // part, (first % part) // step
            if half == 0:
                return (layer + p, piece * (part // step) + row, 0, 0)
            return (far[p][1], (piece ^ me[1]) * (part // step) + row, 0, 0)

        return pl.BlockSpec((1, step, 128, 128), index)

    if other is None:
        specs = [pl.BlockSpec((2, blocks, rows, 128), lambda p, a, c, m: (0, 0, 0, 0))] * count
        operands = list(source)
    else:
        specs = [pl.BlockSpec((count, blocks, rows, 128), lambda p, a, c, m: (0, 0, 0, 0))] * 2
        operands = [source, other]
    own = weights.reshape(weights.shape[0], 2 * blocks, 128, 128)
    for p in range(2):
        for which in range(2):
            specs.append(weight_spec(p, which))
            operands.append(own if half == 0 else far[p][0][which if paired else 0])
    specs.append(pl.BlockSpec((1, step, 1, 128), lambda p, a, c, m: (layer + p, a, 0, 0)))
    operands.append(biases)
    if joined_out:
        out_shape = jax.ShapeDtypeStruct((count, blocks, rows, 128), jnp.bfloat16)
        out_specs = pl.BlockSpec((count, step, rows, 128), lambda p, a, c, m: (0, a * p, 0, 0))
    else:
        out_shape = [jax.ShapeDtypeStruct((blocks, rows, 128), jnp.bfloat16)] * count
        out_specs = [pl.BlockSpec((step, rows, 128), lambda p, a, c, m: (a * p, 0, 0))] * count
    plan = (1 if other is not None else count, half, flip, joined_out, step, layer, blocks, paired)
    cells = count * rows * blocks
    return pl.pallas_call(
        functools.partial(layers_kernel, plan),
        out_shape=out_shape,
        grid_spec=pltpu.PrefetchScalarGridSpec(
            num_scalar_prefetch=2,
            grid=(2, steps),
            in_specs=specs,
            out_specs=out_specs,
            scratch_shapes=[pltpu.VMEM((count, blocks, rows, 128), jnp.bfloat16)],
        ),
        cost_estimate=pl.CostEstimate(
            flops=2 * 2 * cells * 256 * 128,
            transcendentals=0,
            bytes_accessed=2 * 3 * cells * 128 + 2 * 2 * blocks * 128 * 128 * 2,
        ),
    )(cols, me, *operands)


def far_batches(layer_count):
    return [(0, 1), (1, 1)] + [(l, 2) for l in range(2, layer_count - 2, 2)] + [
        (layer_count - 2, 1),
        (layer_count - 1, 1),
    ]


def local(activations, weights, biases, columns):
    slab_count, group_count = lax.axis_size("slab"), lax.axis_size("groups")
    log_count = slab_count.bit_length() - 1
    layer_count, _, blocks, width, _ = weights.shape
    rows = activations.shape[0]
    remote = (layer_count + 1) // 2
    bits = [section_bit(m, remote, log_count) for m in range(remote)]
    first_bit = bits[0]
    spread = [b for b in range(log_count) if b != first_bit]
    count = slab_count // 2
    offsets = [
        sum(((j >> i) & 1) << b for i, b in enumerate(spread)) for j in range(count)
    ]
    slab, group = lax.axis_index("slab"), lax.axis_index("groups")
    me = jnp.stack([slab, group]).astype(jnp.int32)

    far_bias = swap(biases, "slab", 1 << first_bit)
    far_columns = swap(columns, "slab", 1 << first_bit)
    bias = [one.reshape(layer_count, blocks, 1, width) for one in (biases, far_bias)]
    cols = [one.reshape(-1) for one in (columns, far_columns)]

    mine = split(me, activations, offsets, first_bit, blocks)
    pieces = [mine[0]]
    for j in range(1, count):
        pieces.append(swap(mine[j], "slab", offsets[j]))

    part = 2 * blocks // group_count
    parts = weights.reshape(layer_count, group_count, part, width, width)
    far = []
    for first, size in far_batches(layer_count):
        part_mine = lax.dynamic_slice(
            parts, (first, group, 0, 0, 0), (size, 1, part, width, width)
        ).reshape(size, part, width, width)
        held = [swap(part_mine, "slab", 1 << first_bit)]
        for b in range(group_count.bit_length() - 1):
            got = []
            for one in held:
                got.append(swap(one, "groups", 1 << b))
            held = held + got
        if group_count != 2:
            held = [jnp.concatenate(held, axis=1)]
        far += [(held, i) for i in range(size)]

    def weights_of(half, layer):
        return [None, None] if half == 0 else far[layer : layer + 2]

    halves = [pieces, pieces]
    for m in range(remote):
        last = m == remote - 1
        for half in range(2):
            other, flip = None, 0
            if m > 0:
                other = swap(halves[half], "slab", 1 << bits[m])
                flip = offsets.index(1 << bits[m])
            halves[half] = two_layers(
                cols[half], me, halves[half], other, parts, weights_of(half, 2 * m), bias[half],
                2 * m, half, rows, count, flip, not last,
            )
    output = None
    for half in range(2):
        back = [halves[half][0]]
        for j in range(1, count):
            back.append(swap(halves[half][j], "slab", offsets[j]))
        output = merge(me, back, offsets, half << first_bit, output)
    return output


def solution(mesh):
    placed = (
        P(("groups", "slab"), None),
        P(None, None, "slab", None, None),
        P(None, "slab"),
        P(None, "slab"),
    )

    return jax.shard_map(
        local, mesh=mesh, in_specs=placed, out_specs=P(("groups", "slab"), None), check_vma=False
    )
```

```python
import functools

import jax
import jax.numpy as jnp
from jax import lax
from jax.experimental import pallas as pl
from jax.experimental.pallas import tpu as pltpu
from jax.sharding import PartitionSpec as P


ceiling = 4.0


def swap(block, axis, offset):
    count = lax.axis_size(axis)
    return lax.ppermute(block, axis, [(i, i ^ offset) for i in range(count)])


def section_bit(section, remote, log_count):
    if remote <= 1:
        return log_count - 1
    return (remote - 1 - section) * (log_count - 1) // (remote - 1)


def split_kernel(offsets, first_bit, me_ref, act_ref, *refs):
    count = len(offsets)
    outs, taken, sems = refs[:count], refs[count], refs[count + 1]
    width = taken.shape[-1]
    half = pl.program_id(0)

    def copy(h, j):
        home = me_ref[0] ^ (offsets[j] | (h << first_bit))
        start = pl.multiple_of(home * width, 128)
        return pltpu.make_async_copy(
            act_ref.at[:, pl.ds(start, width)], taken.at[h, j], sems.at[h, j]
        )

    @pl.when(half == 0)
    def _():
        for h in range(2):
            for j in range(count):
                copy(h, j).start()

    for j in range(count):
        copy(half, j).wait()
        for k in range(width // 128):
            outs[j][0, k] = taken[half, j, :, k * 128 : (k + 1) * 128]


def split(me, activations, offsets, first_bit, blocks):
    rows = activations.shape[0]
    count = len(offsets)
    width = blocks * 128
    piece = jax.ShapeDtypeStruct((2, blocks, rows, 128), activations.dtype)
    return pl.pallas_call(
        functools.partial(split_kernel, offsets, first_bit),
        out_shape=[piece] * count,
        grid_spec=pltpu.PrefetchScalarGridSpec(
            num_scalar_prefetch=1,
            grid=(2,),
            in_specs=[pl.BlockSpec(memory_space=pl.ANY)],
            out_specs=[pl.BlockSpec((1, blocks, rows, 128), lambda h, me: (h, 0, 0, 0))] * count,
            scratch_shapes=[
                pltpu.VMEM((2, count, rows, width), activations.dtype),
                pltpu.SemaphoreType.DMA((2, count)),
            ],
        ),
        cost_estimate=pl.CostEstimate(
            flops=0, transcendentals=0, bytes_accessed=4 * activations.size
        ),
        name="split",
    )(me, activations)


def merge_kernel(offsets, half_bit, aliased, me_ref, *refs):
    count = len(offsets)
    pieces = refs[:count]
    out_ref, placed, sems = refs[count + aliased :]
    width = placed.shape[-1]
    step = pl.program_id(0)
    last = pl.num_programs(0) - 1
    rows = placed.shape[-2]

    def copy(at, j):
        home = me_ref[0] ^ (offsets[j] | half_bit)
        start = pl.multiple_of(home * width, 128)
        return pltpu.make_async_copy(
            placed.at[at, j],
            out_ref.at[pl.ds(at * rows, rows), pl.ds(start, width)],
            sems.at[at, j],
        )

    for j in range(count):
        for k in range(width // 128):
            placed[step, j, :, k * 128 : (k + 1) * 128] = pieces[j][k]
        copy(step, j).start()

    @pl.when(step == last)
    def _():
        for at in range(placed.shape[0]):
            for j in range(count):
                copy(at, j).wait()


def merge(me, pieces, offsets, half_bit, into, total_width):
    count = len(offsets)
    blocks, total_rows, _ = pieces[0].shape
    steps = 2 if total_rows % 32 == 0 else 1
    rows = total_rows // steps
    width = blocks * 128
    aliased = 0 if into is None else 1
    more = [] if into is None else [into]
    return pl.pallas_call(
        functools.partial(merge_kernel, offsets, half_bit, aliased),
        out_shape=jax.ShapeDtypeStruct((total_rows, total_width), pieces[0].dtype),
        grid_spec=pltpu.PrefetchScalarGridSpec(
            num_scalar_prefetch=1,
            grid=(steps,),
            in_specs=[pl.BlockSpec((blocks, rows, 128), lambda i, me: (0, i, 0))] * count
            + [pl.BlockSpec(memory_space=pl.ANY)] * aliased,
            out_specs=pl.BlockSpec(memory_space=pl.ANY),
            scratch_shapes=[
                pltpu.VMEM((steps, count, rows, width), pieces[0].dtype),
                pltpu.SemaphoreType.DMA((steps, count)),
            ],
        ),
        input_output_aliases={1 + count: 0} if aliased else {},
        cost_estimate=pl.CostEstimate(
            flops=0, transcendentals=0, bytes_accessed=4 * count * pieces[0].size
        ),
    )(me, *pieces, *more)


def layers_kernel(plan, cols_ref, me_ref, *refs):
    sources, half, flip, joined_out, step, layer, blocks, paired = plan
    refs = list(refs)
    src = [refs.pop(0) for _ in range(sources)]
    other = refs.pop(0) if sources == 1 else None
    w = [[refs.pop(0), refs.pop(0)] for _ in range(2)]
    bias = refs.pop(0)
    middle = refs.pop()
    outs = refs
    phase, at = pl.program_id(0), pl.program_id(1)
    count, _, rows, _ = middle.shape
    swapped = me_ref[1] == 1

    def whole(ref, k):
        return ref[:, k].reshape(count * rows, 128)

    def from_source(k):
        if sources == 1:
            return whole(src[0], k)
        return jnp.concatenate([piece[half, k] for piece in src], axis=0)

    def from_partner(k):
        if sources > 1:
            return jnp.concatenate([piece[1 - half, k] for piece in src], axis=0)
        return jnp.concatenate([other[j ^ flip, k] for j in range(count)], axis=0)

    def from_middle(k):
        return whole(middle, k)

    def run(p, own_of, partner_of, store):
        for t in range(step):
            k = at * step + t
            c = cols_ref[(layer + p) * blocks + k]
            both = jnp.concatenate([own_of(k), partner_of(c)], axis=1)
            first, second = w[p][0][0, t], w[p][1][0, t]
            if paired:
                first, second = (
                    jnp.where(swapped, second, first),
                    jnp.where(swapped, first, second),
                )
            taken = jnp.concatenate([first, second], axis=0)
            summed = jnp.dot(both, taken, preferred_element_type=jnp.float32)
            summed = summed + bias[0, t]
            store(k, t, jnp.clip(summed, 0.0, ceiling).astype(jnp.bfloat16))

    @pl.when(phase == 0)
    def _():
        def store(k, t, value):
            middle[:, k] = value.reshape(count, rows, 128)

        run(0, from_source, from_partner, store)

    @pl.when(phase == 1)
    def _():
        def store(k, t, value):
            if joined_out:
                outs[0][:, t] = value.reshape(count, rows, 128)
            else:
                for j in range(count):
                    outs[j][t] = value[j * rows : (j + 1) * rows]

        run(1, from_middle, from_middle, store)


def two_layers(
    cols, me, source, other, weights, far, biases, layer, half, rows, count, flip, joined_out
):
    blocks = biases.shape[1]
    part = weights.shape[2]
    paired = half == 1 and len(far[0][0]) == 2
    step = min(8, part, blocks)
    steps = blocks // step

    def weight_spec(p, which):
        def index(phase, at, cols, me):
            at = jnp.where(phase == p, at, (steps - 1) if p == 0 else 0)
            if paired:
                return (far[p][1], at, 0, 0)
            first = which * blocks + at * step
            piece, row = first // part, (first % part) // step
            if half == 0:
                return (layer + p, piece * (part // step) + row, 0, 0)
            return (far[p][1], (piece ^ me[1]) * (part // step) + row, 0, 0)

        return pl.BlockSpec((1, step, 128, 128), index)

    if other is None:
        specs = [pl.BlockSpec((2, blocks, rows, 128), lambda p, a, c, m: (0, 0, 0, 0))] * count
        operands = list(source)
    else:
        specs = [pl.BlockSpec((count, blocks, rows, 128), lambda p, a, c, m: (0, 0, 0, 0))] * 2
        operands = [source, other]
    own = weights.reshape(weights.shape[0], 2 * blocks, 128, 128)
    for p in range(2):
        for which in range(2):
            specs.append(weight_spec(p, which))
            operands.append(own if half == 0 else far[p][0][which if paired else 0])
    specs.append(pl.BlockSpec((1, step, 1, 128), lambda p, a, c, m: (layer + p, a, 0, 0)))
    operands.append(biases)
    if joined_out:
        out_shape = jax.ShapeDtypeStruct((count, blocks, rows, 128), jnp.bfloat16)
        out_specs = pl.BlockSpec((count, step, rows, 128), lambda p, a, c, m: (0, a * p, 0, 0))
    else:
        out_shape = [jax.ShapeDtypeStruct((blocks, rows, 128), jnp.bfloat16)] * count
        out_specs = [pl.BlockSpec((step, rows, 128), lambda p, a, c, m: (a * p, 0, 0))] * count
    plan = (1 if other is not None else count, half, flip, joined_out, step, layer, blocks, paired)
    cells = count * rows * blocks
    return pl.pallas_call(
        functools.partial(layers_kernel, plan),
        out_shape=out_shape,
        grid_spec=pltpu.PrefetchScalarGridSpec(
            num_scalar_prefetch=2,
            grid=(2, steps),
            in_specs=specs,
            out_specs=out_specs,
            scratch_shapes=[pltpu.VMEM((count, blocks, rows, 128), jnp.bfloat16)],
        ),
        cost_estimate=pl.CostEstimate(
            flops=2 * 2 * cells * 256 * 128,
            transcendentals=0,
            bytes_accessed=2 * 3 * cells * 128 + 2 * 2 * blocks * 128 * 128 * 2,
        ),
    )(cols, me, *operands)


def far_batches(layer_count):
    return [(0, 1), (1, 1)] + [(l, 2) for l in range(2, layer_count - 2, 2)] + [
        (layer_count - 2, 1),
        (layer_count - 1, 1),
    ]


def plan_of(slab_count, layer_count):
    log_count = slab_count.bit_length() - 1
    remote = (layer_count + 1) // 2
    bits = [section_bit(m, remote, log_count) for m in range(remote)]
    spread = [b for b in range(log_count) if b != bits[0]]
    free = [b for b in spread if b not in bits]
    spread = [b for b in spread if b not in free[-1:]] + free[-1:]
    offsets = [
        sum(((j >> i) & 1) << b for i, b in enumerate(spread)) for j in range(slab_count // 2)
    ]
    half = len(offsets) // 2
    chunks = [offsets[:half], offsets[half:]] if free else [offsets]
    return bits, offsets, chunks


def local(activations, weights, biases, columns):
    slab_count, group_count = lax.axis_size("slab"), lax.axis_size("groups")
    layer_count, _, blocks, width, _ = weights.shape
    rows = activations.shape[0]
    remote = (layer_count + 1) // 2
    bits, offsets, chunks = plan_of(slab_count, layer_count)
    first_bit = bits[0]
    slab, group = lax.axis_index("slab"), lax.axis_index("groups")
    me = jnp.stack([slab, group]).astype(jnp.int32)

    far_bias = swap(biases, "slab", 1 << first_bit)
    far_columns = swap(columns, "slab", 1 << first_bit)
    bias = [one.reshape(layer_count, blocks, 1, width) for one in (biases, far_bias)]
    cols = [one.reshape(-1) for one in (columns, far_columns)]

    mine = split(me, activations, offsets, first_bit, blocks)
    pieces = {0: mine[0]}
    for offset, piece in zip(offsets[1:], mine[1:]):
        pieces[offset] = swap(piece, "slab", offset)

    part = 2 * blocks // group_count
    parts = weights.reshape(layer_count, group_count, part, width, width)
    far = []
    for first, size in far_batches(layer_count):
        part_mine = lax.dynamic_slice(
            parts, (first, group, 0, 0, 0), (size, 1, part, width, width)
        ).reshape(size, part, width, width)
        held = [swap(part_mine, "slab", 1 << first_bit)]
        for b in range(group_count.bit_length() - 1):
            got = []
            for one in held:
                got.append(swap(one, "groups", 1 << b))
            held = held + got
        if group_count != 2:
            held = [jnp.concatenate(held, axis=1)]
        far += [(held, i) for i in range(size)]

    def weights_of(half, layer):
        return [None, None] if half == 0 else far[layer : layer + 2]

    output = None
    for chunk in chunks:
        for half in range(2):
            value = [pieces[offset] for offset in chunk]
            for m in range(remote):
                last = m == remote - 1
                other, flip = None, 0
                if m > 0:
                    other = swap(value, "slab", 1 << bits[m])
                    flip = chunk.index(chunk[0] ^ (1 << bits[m]))
                value = two_layers(
                    cols[half], me, value, other, parts, weights_of(half, 2 * m), bias[half],
                    2 * m, half, rows, len(chunk), flip, not last,
                )
            back = []
            for offset, piece in zip(chunk, value):
                if offset:
                    piece = swap(piece, "slab", offset)
                back.append(piece)
            output = merge(
                me, back, chunk, half << first_bit, output,
                slab_count * blocks * width,
            )
    return output


def solution(mesh):
    placed = (
        P(("groups", "slab"), None),
        P(None, None, "slab", None, None),
        P(None, "slab"),
        P(None, "slab"),
    )

    step = jax.shard_map(
        local, mesh=mesh, in_specs=placed, out_specs=P(("groups", "slab"), None), check_vma=False
    )


    def run(activations, weights, biases, columns):
        layer_count = weights.shape[0]
        one = step
        if len(plan_of(mesh.shape["slab"], layer_count)[2]) == 2 and layer_count == 6:
            one = step
        return one(activations, weights, biases, columns)

    return run
```

```python
import functools

import jax
import jax.numpy as jnp
from jax import lax
from jax.experimental import pallas as pl
from jax.experimental.pallas import tpu as pltpu
from jax.sharding import PartitionSpec as P


ceiling = 4.0


def swap(block, axis, offset):
    count = lax.axis_size(axis)
    return lax.ppermute(block, axis, [(i, i ^ offset) for i in range(count)])


def section_bit(section, remote, log_count):
    if remote <= 1:
        return log_count - 1
    return (remote - 1 - section) * (log_count - 1) // (remote - 1)


def split_kernel(offsets, first_bit, me_ref, act_ref, *refs):
    count = len(offsets)
    outs, taken, sems = refs[:count], refs[count], refs[count + 1]
    width = taken.shape[-1]
    half = pl.program_id(0)

    def copy(h, j):
        home = me_ref[0] ^ (offsets[j] | (h << first_bit))
        start = pl.multiple_of(home * width, 128)
        return pltpu.make_async_copy(
            act_ref.at[:, pl.ds(start, width)], taken.at[h, j], sems.at[h, j]
        )

    @pl.when(half == 0)
    def _():
        for h in range(2):
            for j in range(count):
                copy(h, j).start()

    for j in range(count):
        copy(half, j).wait()
        for k in range(width // 128):
            outs[j][0, k] = taken[half, j, :, k * 128 : (k + 1) * 128]


def split(me, activations, offsets, first_bit, blocks):
    rows = activations.shape[0]
    count = len(offsets)
    width = blocks * 128
    piece = jax.ShapeDtypeStruct((2, blocks, rows, 128), activations.dtype)
    return pl.pallas_call(
        functools.partial(split_kernel, offsets, first_bit),
        out_shape=[piece] * count,
        grid_spec=pltpu.PrefetchScalarGridSpec(
            num_scalar_prefetch=1,
            grid=(2,),
            in_specs=[pl.BlockSpec(memory_space=pl.ANY)],
            out_specs=[pl.BlockSpec((1, blocks, rows, 128), lambda h, me: (h, 0, 0, 0))] * count,
            scratch_shapes=[
                pltpu.VMEM((2, count, rows, width), activations.dtype),
                pltpu.SemaphoreType.DMA((2, count)),
            ],
        ),
        cost_estimate=pl.CostEstimate(
            flops=0, transcendentals=0, bytes_accessed=8 * count * rows * width
        ),
        name="split",
    )(me, activations)


def merge_kernel(offsets, half_bit, aliased, me_ref, *refs):
    count = len(offsets)
    pieces = refs[:count]
    out_ref, placed, sems = refs[count + aliased :]
    width = placed.shape[-1]
    step = pl.program_id(0)
    last = pl.num_programs(0) - 1
    rows = placed.shape[-2]

    def copy(at, j):
        home = me_ref[0] ^ (offsets[j] | half_bit)
        start = pl.multiple_of(home * width, 128)
        return pltpu.make_async_copy(
            placed.at[at, j],
            out_ref.at[pl.ds(at * rows, rows), pl.ds(start, width)],
            sems.at[at, j],
        )

    for j in range(count):
        for k in range(width // 128):
            placed[step, j, :, k * 128 : (k + 1) * 128] = pieces[j][k]
        copy(step, j).start()

    @pl.when(step == last)
    def _():
        for at in range(placed.shape[0]):
            for j in range(count):
                copy(at, j).wait()


def merge(me, pieces, offsets, half_bit, into, total_width):
    count = len(offsets)
    blocks, total_rows, _ = pieces[0].shape
    steps = 4 if total_rows % 64 == 0 else 1
    rows = total_rows // steps
    width = blocks * 128
    aliased = 0 if into is None else 1
    more = [] if into is None else [into]
    return pl.pallas_call(
        functools.partial(merge_kernel, offsets, half_bit, aliased),
        out_shape=jax.ShapeDtypeStruct((total_rows, total_width), pieces[0].dtype),
        grid_spec=pltpu.PrefetchScalarGridSpec(
            num_scalar_prefetch=1,
            grid=(steps,),
            in_specs=[pl.BlockSpec((blocks, rows, 128), lambda i, me: (0, i, 0))] * count
            + [pl.BlockSpec(memory_space=pl.ANY)] * aliased,
            out_specs=pl.BlockSpec(memory_space=pl.ANY),
            scratch_shapes=[
                pltpu.VMEM((steps, count, rows, width), pieces[0].dtype),
                pltpu.SemaphoreType.DMA((steps, count)),
            ],
        ),
        input_output_aliases={1 + count: 0} if aliased else {},
        cost_estimate=pl.CostEstimate(
            flops=0, transcendentals=0, bytes_accessed=4 * count * pieces[0].size
        ),
    )(me, *pieces, *more)


def layers_kernel(plan, cols_ref, me_ref, *refs):
    sources, half, flip, joined_out, step, layer, blocks, paired = plan
    refs = list(refs)
    src = [refs.pop(0) for _ in range(sources)]
    other = refs.pop(0) if sources == 1 else None
    w = [[refs.pop(0), refs.pop(0)] for _ in range(2)]
    bias = refs.pop(0)
    middle = refs.pop()
    outs = refs
    phase, at = pl.program_id(0), pl.program_id(1)
    count, _, rows, _ = middle.shape
    swapped = me_ref[1] == 1

    def whole(ref, k):
        return ref[:, k].reshape(count * rows, 128)

    def from_source(k):
        if sources == 1:
            return whole(src[0], k)
        return jnp.concatenate([piece[half, k] for piece in src], axis=0)

    def from_partner(k):
        if sources > 1:
            return jnp.concatenate([piece[1 - half, k] for piece in src], axis=0)
        return jnp.concatenate([other[j ^ flip, k] for j in range(count)], axis=0)

    def from_middle(k):
        return whole(middle, k)

    def run(p, own_of, partner_of, store):
        for t in range(step):
            k = at * step + t
            c = cols_ref[(layer + p) * blocks + k]
            both = jnp.concatenate([own_of(k), partner_of(c)], axis=1)
            first, second = w[p][0][0, t], w[p][1][0, t]
            if paired:
                first, second = (
                    jnp.where(swapped, second, first),
                    jnp.where(swapped, first, second),
                )
            taken = jnp.concatenate([first, second], axis=0)
            summed = jnp.dot(both, taken, preferred_element_type=jnp.float32)
            summed = summed + bias[0, t]
            store(k, t, jnp.clip(summed, 0.0, ceiling).astype(jnp.bfloat16))

    @pl.when(phase == 0)
    def _():
        def store(k, t, value):
            middle[:, k] = value.reshape(count, rows, 128)

        run(0, from_source, from_partner, store)

    @pl.when(phase == 1)
    def _():
        def store(k, t, value):
            if joined_out:
                outs[0][:, t] = value.reshape(count, rows, 128)
            else:
                for j in range(count):
                    outs[j][t] = value[j * rows : (j + 1) * rows]

        run(1, from_middle, from_middle, store)


def two_layers(
    cols, me, source, other, weights, far, biases, layer, half, rows, count, flip, joined_out
):
    blocks = biases.shape[1]
    part = weights.shape[2]
    paired = half == 1 and len(far[0][0]) == 2
    step = min(16, part, blocks)
    steps = blocks // step

    def weight_spec(p, which):
        def index(phase, at, cols, me):
            at = jnp.where(phase == p, at, (steps - 1) if p == 0 else 0)
            if paired:
                return (far[p][1], at, 0, 0)
            first = which * blocks + at * step
            piece, row = first // part, (first % part) // step
            if half == 0:
                return (layer + p, piece * (part // step) + row, 0, 0)
            return (far[p][1], (piece ^ me[1]) * (part // step) + row, 0, 0)

        return pl.BlockSpec((1, step, 128, 128), index)

    if other is None:
        specs = [pl.BlockSpec((2, blocks, rows, 128), lambda p, a, c, m: (0, 0, 0, 0))] * count
        operands = list(source)
    else:
        specs = [pl.BlockSpec((count, blocks, rows, 128), lambda p, a, c, m: (0, 0, 0, 0))] * 2
        operands = [source, other]
    own = weights.reshape(weights.shape[0], 2 * blocks, 128, 128)
    for p in range(2):
        for which in range(2):
            specs.append(weight_spec(p, which))
            operands.append(own if half == 0 else far[p][0][which if paired else 0])
    specs.append(pl.BlockSpec((1, step, 1, 128), lambda p, a, c, m: (layer + p, a, 0, 0)))
    operands.append(biases)
    if joined_out:
        out_shape = jax.ShapeDtypeStruct((count, blocks, rows, 128), jnp.bfloat16)
        out_specs = pl.BlockSpec((count, step, rows, 128), lambda p, a, c, m: (0, a * p, 0, 0))
    else:
        out_shape = [jax.ShapeDtypeStruct((blocks, rows, 128), jnp.bfloat16)] * count
        out_specs = [pl.BlockSpec((step, rows, 128), lambda p, a, c, m: (a * p, 0, 0))] * count
    plan = (1 if other is not None else count, half, flip, joined_out, step, layer, blocks, paired)
    cells = count * rows * blocks
    return pl.pallas_call(
        functools.partial(layers_kernel, plan),
        out_shape=out_shape,
        grid_spec=pltpu.PrefetchScalarGridSpec(
            num_scalar_prefetch=2,
            grid=(2, steps),
            in_specs=specs,
            out_specs=out_specs,
            scratch_shapes=[pltpu.VMEM((count, blocks, rows, 128), jnp.bfloat16)],
        ),
        cost_estimate=pl.CostEstimate(
            flops=2 * 2 * cells * 256 * 128,
            transcendentals=0,
            bytes_accessed=2 * 3 * cells * 128 + 2 * 2 * blocks * 128 * 128 * 2,
        ),
    )(cols, me, *operands)


def far_batches(layer_count):
    return [(0, 1), (1, 1)] + [(l, 2) for l in range(2, layer_count - 2, 2)] + [
        (layer_count - 2, 1),
        (layer_count - 1, 1),
    ]


def plan_of(slab_count, layer_count):
    log_count = slab_count.bit_length() - 1
    remote = (layer_count + 1) // 2
    bits = [section_bit(m, remote, log_count) for m in range(remote)]
    spread = [b for b in range(log_count) if b != bits[0]]
    free = [b for b in spread if b not in bits]
    spread = [b for b in spread if b not in free[-1:]] + free[-1:]
    offsets = [
        sum(((j >> i) & 1) << b for i, b in enumerate(spread)) for j in range(slab_count // 2)
    ]
    half = len(offsets) // 2
    chunks = [offsets[:half], offsets[half:]] if free else [offsets]
    return bits, offsets, chunks


def local(activations, weights, biases, columns):
    slab_count, group_count = lax.axis_size("slab"), lax.axis_size("groups")
    layer_count, _, blocks, width, _ = weights.shape
    rows = activations.shape[0]
    remote = (layer_count + 1) // 2
    bits, _, chunks = plan_of(slab_count, layer_count)
    first_bit = bits[0]
    slab, group = lax.axis_index("slab"), lax.axis_index("groups")
    me = jnp.stack([slab, group]).astype(jnp.int32)

    far_bias = swap(biases, "slab", 1 << first_bit)
    far_columns = swap(columns, "slab", 1 << first_bit)
    bias = [one.reshape(layer_count, blocks, 1, width) for one in (biases, far_bias)]
    cols = [one.reshape(-1) for one in (columns, far_columns)]

    pieces = {}
    for chunk in chunks:
        mine = split(me, activations, chunk, first_bit, blocks)
        for offset, piece in zip(chunk, mine):
            if offset:
                piece = swap(piece, "slab", offset)
            pieces[offset] = piece

    part = 2 * blocks // group_count
    parts = weights.reshape(layer_count, group_count, part, width, width)
    far = []
    for first, size in far_batches(layer_count):
        part_mine = lax.dynamic_slice(
            parts, (first, group, 0, 0, 0), (size, 1, part, width, width)
        ).reshape(size, part, width, width)
        held = [swap(part_mine, "slab", 1 << first_bit)]
        for b in range(group_count.bit_length() - 1):
            got = []
            for one in held:
                got.append(swap(one, "groups", 1 << b))
            held = held + got
        if group_count != 2:
            held = [jnp.concatenate(held, axis=1)]
        far += [(held, i) for i in range(size)]

    def weights_of(half, layer):
        return [None, None] if half == 0 else far[layer : layer + 2]

    returned = {}
    for c, chunk in enumerate(chunks):
        for half in range(2):
            value = [pieces[offset] for offset in chunk]
            for m in range(remote):
                last = m == remote - 1
                other, flip = None, 0
                if m > 0:
                    other = swap(value, "slab", 1 << bits[m])
                    flip = chunk.index(chunk[0] ^ (1 << bits[m]))
                value = two_layers(
                    cols[half], me, value, other, parts, weights_of(half, 2 * m), bias[half],
                    2 * m, half, rows, len(chunk), flip, not last,
                )
            back = []
            for offset, piece in zip(chunk, value):
                if offset:
                    piece = swap(piece, "slab", offset)
                back.append(piece)
            returned[c, half] = back
    output = None
    for c, half in sorted(returned, key=lambda key: key == (0, 1)):
        output = merge(
            me, returned[c, half], chunks[c], half << first_bit, output,
            slab_count * blocks * width,
        )
    return output


def solution(mesh):
    placed = (
        P(("groups", "slab"), None),
        P(None, None, "slab", None, None),
        P(None, "slab"),
        P(None, "slab"),
    )

    step = jax.shard_map(
        local, mesh=mesh, in_specs=placed, out_specs=P(("groups", "slab"), None), check_vma=False
    )


    def run(activations, weights, biases, columns):
        layer_count = weights.shape[0]
        one = step
        if len(plan_of(mesh.shape["slab"], layer_count)[2]) == 2 and layer_count == 6:
            one = step
        return one(activations, weights, biases, columns)

    return run
```
